512 devices in a mesh: prow: 32 (over y_hi, z), pcol: 16 (over y_lo, x, core).
Axes of the slice: x: 4, y: 4 (y_hi: 2, y_lo: 2; y = y_hi * 2 + y_lo), z: 16, core: 2. Of those that a mesh axis runs over, the one named last changes fastest.
Arguments:
- ainv: bfloat16 [3, 32, 256, 6, 16, 256], P(None, 'prow', None, None, 'pcol'), may hold values from -0.0390625 to 0.0390625
- panel: bfloat16 [6, 16, 256, 1536], P(None, 'pcol', None, 'prow'), may hold values from -6 to 6
- structure: int32 [4, 96], replicated, may hold values 0 or 1
- widths: int32 [4], replicated, may hold values from 1 to 512, 1536 in all
Outputs:
- inverse_panel: bfloat16 [3, 32, 256, 1536], P(None, 'prow', None, 'pcol')
The draws below stay inside these ranges and needn't reach their ends.
Inputs may be any that keep to these rules, and one draw needn't show every extreme that they name: Supernode k owns the next widths[k] columns; the widths sum to 1536 and the widest is exactly 512.
All inputs are finite; a program needn't handle non-finite values.
Results may differ from the reference program's by a relative error of at most 0.001.
Values may be sent and summed in bfloat16 or wider, within the bound.
A program may use at most 64 MiB of HBM per device.

```python
import math
import jax
import jax.numpy as jnp
import numpy as np
from jax import lax

B = 256
SUP = 4
WT = 1536
WMAX = 512
BR = 3
NB = 96
BC = 6
N_PROW = 32
N_PCOL = 16


def touch_ends(drawn, rng, least, largest):
    longest = drawn.shape.index(max(drawn.shape))
    spots = []
    for shift in (0, 1):
        where = [jax.random.randint(jax.random.fold_in(rng, axis), (), 0, length) for axis, length in enumerate(drawn.shape)]
        where[longest] = (where[longest] + shift) % drawn.shape[longest]
        spots.append(tuple(where))
    return drawn.at[spots[0]].set(least).at[spots[1]].set(largest)


def block_levels(rng, dims, split, least, high):
    gain, own = 1.0, jax.random.fold_in(rng, 6)
    for axis_at, blocks in split:
        steps = jnp.exp(jax.random.uniform(jax.random.fold_in(own, axis_at), (blocks,), jnp.float32, least / len(split), high / len(split)))
        gain = gain * jnp.repeat(steps, dims[axis_at] // blocks).reshape([-1 if axis == axis_at else 1 for axis in range(len(dims))])
    return gain


def split_up(count, total, most, slope):
    loads = [(1 << 20) // math.isqrt(rank ** slope) + 1 for rank in range(2, count + 1)]
    spare, holding = total - most - (count - 1), [1] * (count - 1)
    while spare > 0:
        movable = [i for i in range(count - 1) if holding[i] < most]
        pool, budget = sum([loads[i] for i in movable]), spare
        for i in movable:
            more = min(most - holding[i], max(1, budget * loads[i] // pool), spare)
            holding[i] = holding[i] + more
            spare = spare - more
    return np.array([most] + holding)


def uneven(key, amount, total, limit, slope):
    if amount == 2:
        one = jax.random.randint(key, (), max(1, total - limit), min(limit, total - 1) + 1)
        return jnp.stack([one, total - one])
    lengths = jnp.asarray(split_up(amount, total, limit, slope), jnp.int32)
    pairs = (amount - 1) // 2
    giver, receiver = lengths[1:1 + 2 * pairs:2], lengths[2:2 + 2 * pairs:2]
    slack = jnp.minimum(giver - 1, limit - receiver)
    moved = jax.random.randint(jax.random.fold_in(key, 1), (pairs,), 0, 1 << 20) % (slack + 1)
    lengths = lengths.at[1:1 + 2 * pairs:2].set(giver - moved).at[2:2 + 2 * pairs:2].set(receiver + moved)
    return lengths[jax.random.permutation(jax.random.fold_in(key, 2), amount)]


def noise(rng, dims, deviation, reach, split=(), kind=jnp.bfloat16):
    drawn = deviation * jax.random.normal(rng, dims, jnp.float32)
    if split:
        drawn = drawn * block_levels(rng, dims, split, -0.22, 0.18)
    return jnp.clip(drawn, -reach, reach).astype(kind)


def setup_inputs(seed: int = 0) -> dict:
    key_list = jax.random.split(jax.random.key(seed), 5)
    return {
        "ainv": noise(key_list[0], (BR, N_PROW, B, BC, N_PCOL, B), (NB * B) ** -0.5, 0.0390625, ((1, 32), (4, 16))),
        "panel": noise(key_list[1], (BC, N_PCOL, B, WT), 1.0, 6.0, ((1, 16), (3, 32))),
        "structure": touch_ends((jax.random.randint(key_list[2], (SUP, NB), 0, 2) < 1).astype(jnp.int32), jax.random.fold_in(key_list[2], 1), 0, 1),
        "widths": uneven(key_list[3], SUP, WT, WMAX, 1).astype(jnp.int32),
    }


def owner_columns(widths, count):
    ends = jnp.cumsum(widths, dtype=jnp.int32)
    columns = jnp.arange(count, dtype=jnp.int32)
    return jnp.sum((columns[:, None] >= ends[None, :]).astype(jnp.int32), axis=1)


def reference(ainv, panel, structure, widths):
    blocks = structure.shape[1]
    order = blocks * B
    amat = ainv.reshape(order, order)
    pmat = panel.reshape(order, WT)
    owner = owner_columns(widths, WT)
    onehot = (owner[:, None] == jnp.arange(SUP, dtype=jnp.int32)[None, :]).astype(jnp.float32)
    block_keep = jnp.dot(structure.T.astype(jnp.float32), onehot.T, precision=lax.Precision.HIGHEST)
    keep = jnp.repeat(block_keep, B, axis=0)
    masked = (pmat.astype(jnp.float32) * keep).astype(jnp.bfloat16)
    product = jnp.dot(amat.astype(jnp.float32), masked.astype(jnp.float32), precision=lax.Precision.HIGHEST)
    result = (-(product * keep)).astype(jnp.bfloat16)
    return result.reshape(BR, N_PROW, B, WT)
```

```python
import jax
import jax.numpy as jnp
from jax import lax
from jax.experimental import pallas as pl
from jax.experimental.pallas import tpu as pltpu
from jax.sharding import PartitionSpec as P

MESH = pl.DeviceIdType.MESH
NZ, NY, NX, NK = 16, 2, 4, 2


def column_keep(struct_ref, widths_ref, block, first, shape, axis):
    columns = first + lax.broadcasted_iota(jnp.int32, shape, axis)
    keep = jnp.zeros(shape, jnp.int32)
    low = jnp.int32(0)
    for k in range(struct_ref.shape[0]):
        high = low + widths_ref[k]
        inside = (columns >= low) & (columns < high)
        keep = keep + jnp.where(inside, struct_ref[k, block], 0)
        low = high
    return keep.astype(jnp.float32)


def kernel(struct_ref, widths_ref, p_ref, a_hbm, o_ref, abuf, pbuf, part, crecv, yrecv, xrecv, half,
           a_sem, pair_s, pair_r, up_s, up_r, dn_s, dn_r, core_s, core_r, y_s, y_r, x_s, x_r):
    row = lax.axis_index("prow")
    col = lax.axis_index("pcol")
    yh, z = row // NZ, row % NZ
    yl, x, k = col // (NX * NK), (col // NK) % NX, col % NK

    def dev(yh=yh, z=z, yl=yl, x=x, k=k):
        return (yh * NZ + z, (yl * NX + x) * NK + k)

    def z_at(step):
        return lax.rem(z + step + NZ, NZ)

    up_dev, dn_dev = dev(z=z_at(1)), dev(z=z_at(-1))
    pair_dev, core_dev, y_dev = dev(yh=1 - yh), dev(k=1 - k), dev(yl=1 - yl)
    x_devs = [dev(x=lax.rem(x + d, NX), k=kk) for d in range(1, NX) for kk in range(NK)]

    barrier = pltpu.get_barrier_semaphore()
    partners = [up_dev, dn_dev, pair_dev, core_dev, y_dev] + x_devs
    for d in partners:
        pl.semaphore_signal(barrier, inc=1, device_id=d, device_id_type=MESH)
    a_copy = pltpu.make_async_copy(a_hbm, abuf, a_sem)
    a_copy.start()
    blocks = p_ref.shape[0]
    npcol = lax.axis_size("pcol")
    for b in range(blocks):
        keep = column_keep(struct_ref, widths_ref, b * npcol + col, row * 48, (48, 256), 0)
        pbuf[z, yh, b] = (p_ref[b].astype(jnp.float32) * keep).astype(jnp.bfloat16)
    pl.semaphore_wait(barrier, len(partners))

    def remote(src, dst, send, recv, device):
        return pltpu.make_async_remote_copy(
            src_ref=src, dst_ref=dst, send_sem=send, recv_sem=recv, device_id=device, device_id_type=MESH)

    def pair():
        return remote(pbuf.at[z, yh], pbuf.at[z, yh], pair_s, pair_r, pair_dev)

    def pair_in():
        return remote(pbuf.at[z, 1 - yh], pbuf.at[z, 1 - yh], pair_s, pair_r, pair_dev)

    def up(s, q, zz):
        y = yh if q == 0 else 1 - yh
        return remote(pbuf.at[zz, y], pbuf.at[zz, y], up_s.at[s, q], up_r.at[s, q], up_dev)

    def dn(s, q, zz):
        y = yh if q == 0 else 1 - yh
        return remote(pbuf.at[zz, y], pbuf.at[zz, y], dn_s.at[s, q], dn_r.at[s, q], dn_dev)

    def products(zs):
        n = len(zs)
        for a in range(abuf.shape[0]):
            total = None
            for b in range(blocks):
                rows = [pbuf[zz, :, b].reshape(96, 256) for zz in zs]
                lhs = rows[0] if n == 1 else jnp.concatenate(rows, axis=0)
                term = lax.dot_general(lhs, abuf[a, b], (((1,), (1,)), ((), ())), preferred_element_type=jnp.float32)
                total = term if total is None else total + term
            for i, zz in enumerate(zs):
                piece = total[96 * i:96 * i + 96].reshape(2, 48, 256)
                if a == 0:
                    part[zz, 0, :, :, 0:256] = piece
                elif a == 1:
                    part[zz, 0, :, :, 256:384] = piece[:, :, 0:128]
                    part[zz, 1, :, :, 0:128] = piece[:, :, 128:256]
                else:
                    part[zz, 1, :, :, 128:384] = piece

    def core(t, zz):
        return remote(part.at[zz, 1 - k], crecv.at[zz], core_s.at[t], core_r.at[t], core_dev)

    def ycopy(t, zz):
        return remote(part.at[zz, k, 1 - yl], yrecv.at[zz], y_s.at[t], y_r.at[t], y_dev)

    def xcopy(t, zz):
        xo, ko, h = zz // 4, (zz // 2) % 2, zz % 2
        slot = lax.rem(x - xo + NX, NX) * NK + lax.rem(k - ko + NK, NK)
        return remote(part.at[zz, k, yl], xrecv.at[slot, h], x_s.at[t], x_r.at[slot, h], dev(x=xo, k=ko))

    def mine(zz):
        return zz // 2 == x * 2 + k

    def stage_core(t, zz):
        core(t, zz).start()

    def stage_y(t, zz):
        core(t, zz).wait_recv()
        part[zz, k] = part[zz, k] + crecv[zz]
        ycopy(t, zz).start()

    def stage_x(t, zz):
        ycopy(t, zz).wait_recv()
        part[zz, k, yl] = part[zz, k, yl] + yrecv[zz]

        @pl.when(jnp.logical_not(mine(zz)))
        def _():
            xcopy(t, zz).start()

    def at(s):
        if isinstance(s, int) and s == 0:
            return [(0, z)]
        if isinstance(s, int) and s == 8:
            return [(15, z_at(8))]
        return [(2 * s - 1, z_at(-s)), (2 * s, z_at(s))]

    def step(s):
        last, fwd = isinstance(s, int) and s == 8, not (isinstance(s, int) and s >= 7)
        for q in range(2):
            if not (last and q == 1):
                up(s, q, z_at(-s)).wait_recv()
                if fwd or (not last and q == 0):
                    up(s + 1, q, z_at(-s)).start()
            if not (last and q == 0):
                dn(s, q, z_at(s)).wait_recv()
                if fwd or (not last and q == 1):
                    dn(s + 1, q, z_at(s)).start()
            if q == 0:
                for t, zz in at(s - 1):
                    stage_y(t, zz)
        products([zz for _, zz in at(s)])
        for t, zz in at(s):
            stage_core(t, zz)
        if not (isinstance(s, int) and s < 2):
            for t, zz in at(s - 2 if not isinstance(s, int) else s - 2):
                stage_x(t, zz)

    pair().start()
    up(1, 0, z).start()
    dn(1, 0, z).start()
    a_copy.wait()
    pair_in().wait_recv()
    up(1, 1, z).start()
    dn(1, 1, z).start()
    products([z])
    stage_core(0, z)
    step(1)
    step(2)

    @pl.loop(3, 7)
    def _(s):
        step(s)

    step(7)
    step(8)
    for t, zz in at(7):
        stage_x(t, zz)
    for t, zz in at(8):
        stage_y(t, zz)
    for t, zz in at(8):
        stage_x(t, zz)

    for h in range(2):
        zz = 4 * x + 2 * k + h
        for slot in range(1, 8):
            remote(xrecv.at[slot, h], xrecv.at[slot, h], x_s.at[0], x_r.at[slot, h], core_dev).wait_recv()
        half[k] = part[zz, k, yl] + xrecv[2, h] + xrecv[4, h] + xrecv[6, h]
        half[1 - k] = xrecv[1, h] + xrecv[3, h] + xrecv[5, h] + xrecv[7, h]
        nprow = lax.axis_size("prow")
        lanes = [half[0, :, 0:256], jnp.concatenate([half[0, :, 256:384], half[1, :, 0:128]], axis=1), half[1, :, 128:384]]
        for a in range(3):
            keep = column_keep(struct_ref, widths_ref, a * nprow + row, col * 96 + 48 * h, (48, 256), 0)
            o_ref[a, 48 * h:48 * h + 48, :] = (-(lanes[a] * keep)).astype(jnp.bfloat16)

    pair().wait_send()
    for s in range(1, 9):
        for q in range(2):
            if s < 8 or q == 0:
                up(s, q, z).wait_send()
            if s < 8 or q == 1:
                dn(s, q, z).wait_send()
    for s in range(9):
        for t, zz in at(s):
            core(t, zz).wait_send()
            ycopy(t, zz).wait_send()

            @pl.when(jnp.logical_not(mine(zz)))
            def _(t=t, zz=zz):
                xcopy(t, zz).wait_send()


def body(ainv, panel, structure, widths):
    a = ainv[:, 0, :, :, 0, :].transpose(0, 2, 1, 3)
    p = panel[:, 0].transpose(0, 2, 1)
    dma = pltpu.SemaphoreType.DMA
    f32, bf16 = jnp.float32, jnp.bfloat16
    out = pl.pallas_call(
        kernel,
        out_shape=jax.ShapeDtypeStruct((3, 96, 256), bf16),
        in_specs=[pl.BlockSpec(memory_space=pltpu.SMEM), pl.BlockSpec(memory_space=pltpu.SMEM),
                  pl.BlockSpec(memory_space=pltpu.VMEM), pl.BlockSpec(memory_space=pl.ANY)],
        out_specs=pl.BlockSpec(memory_space=pltpu.VMEM),
        scratch_shapes=[
            pltpu.VMEM((3, 6, 256, 256), bf16),
            pltpu.VMEM((NZ, NY, 6, 48, 256), bf16),
            pltpu.VMEM((NZ, 2, 2, 48, 384), f32),
            pltpu.VMEM((NZ, 2, 48, 384), f32),
            pltpu.VMEM((NZ, 48, 384), f32),
            pltpu.VMEM((8, 2, 48, 384), f32),
            pltpu.VMEM((2, 48, 384), f32),
            dma, dma, dma, dma((9, 2)), dma((9, 2)), dma((9, 2)), dma((9, 2)),
            dma((16,)), dma((16,)), dma((16,)), dma((16,)), dma((16,)), dma((8, 2)),
        ],
        compiler_params=pltpu.CompilerParams(
            collective_id=0, has_side_effects=True, vmem_limit_bytes=48 << 20),
        name="gather_multiply_scatter",
    )(structure, widths, p, a)
    return out.transpose(0, 2, 1)[:, None]


def solution(mesh):
    in_specs = (P(None, "prow", None, None, "pcol", None), P(None, "pcol", None, "prow"), P(), P())
    out_specs = P(None, "prow", None, "pcol")
    return jax.shard_map(body, mesh=mesh, in_specs=in_specs, out_specs=out_specs, check_vma=False)
```

```python
import jax
import jax.numpy as jnp
from jax import lax
from jax.experimental import pallas as pl
from jax.experimental.pallas import tpu as pltpu
from jax.sharding import PartitionSpec as P

MESH = pl.DeviceIdType.MESH
NZ, NY, NX, NK = 16, 2, 4, 2


def supernode_masks(widths_ref, first, shape):
    columns = first + lax.broadcasted_iota(jnp.int32, shape, 0)
    masks, low = [], jnp.int32(0)
    for k in range(widths_ref.shape[0]):
        high = low + widths_ref[k]
        masks.append((columns >= low) & (columns < high))
        low = high
    return masks


def keep_of(masks, struct_ref, block):
    keep = jnp.zeros(masks[0].shape, jnp.int32)
    for k, mask in enumerate(masks):
        keep = keep + jnp.where(mask, struct_ref[k, block], 0)
    return keep.astype(jnp.float32)


def kernel(struct_hbm, widths_hbm, p_hbm, a_hbm, o_ref, struct_ref, widths_ref, own, abuf, pbuf, part, crecv, xrecv, yrecv,
           frecv, half, in_sem, pair_s, pair_r, up_s, up_r, dn_s, dn_r, late_s, late_r, core_s, core_r, x_s, x_r, y_s, y_r,
           f_s, f_r):
    row = lax.axis_index("prow")
    col = lax.axis_index("pcol")
    nprow, npcol = lax.axis_size("prow"), lax.axis_size("pcol")
    yh, z = row // NZ, row % NZ
    yl, x, k = col // (NX * NK), (col // NK) % NX, col % NK

    def dev(yh=yh, z=z, yl=yl, x=x, k=k):
        return (yh * NZ + z, (yl * NX + x) * NK + k)

    def z_at(step):
        return lax.rem(z + step + NZ, NZ)

    loads = [pltpu.make_async_copy(src, dst, in_sem.at[i]) for i, (src, dst) in enumerate(
        [(struct_hbm, struct_ref), (widths_hbm, widths_ref), (p_hbm, own), (a_hbm, abuf)])]
    for load in loads:
        load.start()
    up_dev, dn_dev = dev(z=z_at(1)), dev(z=z_at(-1))
    pair_dev, core_dev, y_dev = dev(yh=1 - yh), dev(k=1 - k), dev(yl=1 - yl)
    partners = [up_dev, dn_dev, pair_dev, core_dev, y_dev] + [dev(x=lax.rem(x + d, NX)) for d in range(1, NX)]
    barrier = pltpu.get_barrier_semaphore()
    for d in partners:
        pl.semaphore_signal(barrier, inc=1, device_id=d, device_id_type=MESH)
    for load in loads[:3]:
        load.wait()
    masks = supernode_masks(widths_ref, row * 48, (48, 256))
    for b in range(6):
        keep = keep_of(masks, struct_ref, b * npcol + col)
        pbuf[z, yh, b] = (own[b].astype(jnp.float32) * keep).astype(jnp.bfloat16)
    pl.semaphore_wait(barrier, len(partners))

    def remote(src, dst, send, recv, device):
        return pltpu.make_async_remote_copy(
            src_ref=src, dst_ref=dst, send_sem=send, recv_sem=recv, device_id=device, device_id_type=MESH)

    def piece(zz, y, second):
        return pbuf.at[zz, y, pl.ds(3 if second else 0, 3)]

    def ring(sems, device):
        def message(s, h, zz):
            ref = piece(zz, 1 - yh if h == 2 else yh, h == 1)
            return remote(ref, ref, sems[0].at[s, h], sems[1].at[s, h], device)
        return message

    up, dn = ring((up_s, up_r), up_dev), ring((dn_s, dn_r), dn_dev)

    def pair(y):
        return remote(piece(z, y, False), piece(z, y, False), pair_s, pair_r, pair_dev)

    def late(t, zz, y):
        return remote(piece(zz, y, True), piece(zz, y, True), late_s.at[t], late_r.at[t], pair_dev)

    def products(zs):
        n = len(zs)
        for a in range(3):
            total = None
            for b in range(6):
                rows = [pbuf[zz, :, b].reshape(96, 256) for zz in zs]
                lhs = rows[0] if n == 1 else jnp.concatenate(rows, axis=0)
                term = lax.dot_general(lhs, abuf[a, b], (((1,), (1,)), ((), ())), preferred_element_type=jnp.float32)
                total = term if total is None else total + term
            for i, zz in enumerate(zs):
                got = total[96 * i:96 * i + 96].reshape(2, 48, 256)
                if a == 0:
                    part[zz, 0, :, :, 0:256] = got
                elif a == 1:
                    part[zz, 0, :, :, 256:384] = got[:, :, 0:128]
                    part[zz, 1, :, :, 0:128] = got[:, :, 128:256]
                else:
                    part[zz, 1, :, :, 128:384] = got

    def core(t, zz):
        return remote(part.at[zz, 1 - k], crecv.at[zz], core_s.at[t], core_r.at[t], core_dev)

    def xcopy(t, zz):
        slot = lax.rem(x - zz // 4 + NX, NX) - 1
        return remote(part.at[zz, k], xrecv.at[slot, zz % 4], x_s.at[t], x_r.at[slot, zz % 4], dev(x=zz // 4))

    def xcopy_in(slot, zz):
        return remote(part.at[zz, k], xrecv.at[slot, zz % 4], x_s.at[0], x_r.at[slot, zz % 4], core_dev)

    def ycopy(zz):
        return remote(part.at[zz, k, 1 - yl], yrecv.at[zz % 4], y_s.at[zz % 4], y_r.at[zz % 4], y_dev)

    def fcopy(zz):
        return remote(part.at[zz, k, yl], frecv.at[zz % 2], f_s.at[zz % 2], f_r.at[zz % 2], core_dev)

    def stage_x(t, zz):
        core(t, zz).wait_recv()
        part[zz, k] = part[zz, k] + crecv[zz]

        @pl.when(zz // 4 != x)
        def _():
            xcopy(t, zz).start()

    def stage_y(t, zz):
        @pl.when(zz // 4 == x)
        def _():
            for slot in range(3):
                xcopy_in(slot, zz).wait_recv()
            j = zz % 4
            part[zz, k] = part[zz, k] + xrecv[0, j] + xrecv[1, j] + xrecv[2, j]
            ycopy(zz).start()

    def stage_f(t, zz):
        @pl.when(zz // 4 == x)
        def _():
            ycopy(zz).wait_recv()
            part[zz, k, yl] = part[zz, k, yl] + yrecv[zz % 4]

            @pl.when((zz // 2) % 2 != k)
            def _():
                fcopy(zz).start()

    def items(s):
        if isinstance(s, int):
            if s == 0:
                return [(0, z)]
            if s == 8:
                return [(15, z_at(8))]
        return [(2 * s - 1, z_at(-s)), (2 * s, z_at(s))]

    def run(stage, s):
        if isinstance(s, int):
            for t, zz in items(s) if s >= 0 else []:
                stage(t, zz)
            return
        for t, zz in items(s):
            @pl.when(t >= 0)
            def _(t=t, zz=zz):
                stage(t, lax.rem(zz + NZ, NZ))

    def multiply(s):
        for t, zz in items(s):
            late(t, zz, 1 - yh).wait_recv()
        products([zz for _, zz in items(s)])
        for t, zz in items(s):
            core(t, zz).start()

    def when(s, do):
        if isinstance(s, int):
            if s < 7:
                do()
        else:
            pl.when(s < 7)(do)

    def step(s):
        last = isinstance(s, int) and s == 8
        below, above = z_at(-s), z_at(s)
        up(s, 0, below).wait_recv()
        if not last:
            up(s + 1, 0, below).start()
            dn(s, 0, above).wait_recv()
            when(s, dn(s + 1, 0, above).start)
        multiply(s - 1)
        if not last:
            up(s, 1, below).wait_recv()
            when(s, up(s + 1, 1, below).start)
        dn(s, 1, above).wait_recv()
        if not last:
            dn(s + 1, 1, above).start()
        for t, zz in items(s):
            late(t, zz, yh).start()
        run(stage_x, s - 2)
        up(s, 2, below).wait_recv()
        if not last:
            up(s + 1, 2, below).start()
            dn(s, 2, above).wait_recv()
            when(s, dn(s + 1, 2, above).start)
        run(stage_y, s - 4)
        run(stage_f, s - 5)

    for h in range(2):
        up(1, h, z).start()
        dn(1, h, z).start()
        if h == 0:
            pair(yh).start()
    late(0, z, yh).start()
    loads[3].wait()
    pair(1 - yh).wait_recv()
    up(1, 2, z).start()
    dn(1, 2, z).start()
    step(1)

    @pl.loop(2, 8)
    def _(s):
        step(s)

    step(8)
    multiply(8)
    run(stage_x, 7)
    run(stage_y, 5)
    run(stage_f, 4)
    run(stage_x, 8)
    run(stage_y, 6)
    run(stage_f, 5)
    run(stage_y, 7)
    run(stage_f, 6)
    run(stage_y, 8)
    run(stage_f, 7)
    run(stage_f, 8)

    masks = supernode_masks(widths_ref, col * 96, (96, 256))
    keeps = [keep_of(masks, struct_ref, a * nprow + row) for a in range(3)]
    for h in range(2):
        zz = 4 * x + 2 * k + h
        fcopy(zz).wait_recv()
        half[k] = part[zz, k, yl]
        half[1 - k] = frecv[h]
        lanes = [half[0, :, 0:256], jnp.concatenate([half[0, :, 256:384], half[1, :, 0:128]], axis=1), half[1, :, 128:384]]
        for a in range(3):
            o_ref[a, 48 * h:48 * h + 48, :] = (-(lanes[a] * keeps[a][48 * h:48 * h + 48])).astype(jnp.bfloat16)

    pair(yh).wait_send()

    @pl.loop(1, 8)
    def _(s):
        for h in range(3):
            up(s, h, z).wait_send()
            dn(s, h, z).wait_send()

    up(8, 0, z).wait_send()
    up(8, 2, z).wait_send()
    dn(8, 1, z).wait_send()

    @pl.loop(0, 16)
    def _(t):
        s = (t + 1) // 2
        zz = lax.rem(z + jnp.where(t % 2 == 1, -s, s) + NZ, NZ)
        late(t, zz, yh).wait_send()
        core(t, zz).wait_send()

        @pl.when(zz // 4 != x)
        def _():
            xcopy(t, zz).wait_send()

    for j in range(4):
        ycopy(4 * x + j).wait_send()
    for h in range(2):
        fcopy(4 * x + 2 * (1 - k) + h).wait_send()


def body(ainv, panel, structure, widths):
    a = ainv[:, 0, :, :, 0, :].transpose(0, 2, 1, 3)
    p = panel[:, 0].transpose(0, 2, 1)
    dma, vmem = pltpu.SemaphoreType.DMA, pltpu.VMEM
    f32, bf16 = jnp.float32, jnp.bfloat16
    out = pl.pallas_call(
        kernel,
        out_shape=jax.ShapeDtypeStruct((3, 96, 256), bf16),
        in_specs=[pl.BlockSpec(memory_space=pl.ANY)] * 4,
        out_specs=pl.BlockSpec(memory_space=vmem),
        scratch_shapes=[
            pltpu.SMEM((4, 96), jnp.int32), pltpu.SMEM((4,), jnp.int32), vmem((6, 48, 256), bf16),
            vmem((3, 6, 256, 256), bf16),
            vmem((NZ, NY, 6, 48, 256), bf16),
            vmem((NZ, 2, 2, 48, 384), f32),
            vmem((NZ, 2, 48, 384), f32),
            vmem((3, 4, 2, 48, 384), f32),
            vmem((4, 48, 384), f32),
            vmem((2, 48, 384), f32),
            vmem((2, 48, 384), f32),
            dma((4,)), dma, dma, dma((9, 3)), dma((9, 3)), dma((9, 3)), dma((9, 3)),
            dma((16,)), dma((16,)), dma((16,)), dma((16,)), dma((16,)), dma((3, 4)),
            dma((4,)), dma((4,)), dma((2,)), dma((2,)),
        ],
        compiler_params=pltpu.CompilerParams(
            collective_id=0, has_side_effects=True, vmem_limit_bytes=60 << 20),
        name="gather_multiply_scatter",
    )(structure, widths, p, a)
    return out.transpose(0, 2, 1)[:, None]


def solution(mesh):
    in_specs = (P(None, "prow", None, None, "pcol", None), P(None, "pcol", None, "prow"), P(), P())
    out_specs = P(None, "prow", None, "pcol")
    return jax.shard_map(body, mesh=mesh, in_specs=in_specs, out_specs=out_specs, check_vma=False)
```

```python
import jax
import jax.numpy as jnp
from jax import lax
from jax.experimental import pallas as pl
from jax.experimental.pallas import tpu as pltpu
from jax.sharding import PartitionSpec as P

MESH = pl.DeviceIdType.MESH
NZ, NY, NX, NK = 16, 2, 4, 2


def supernode_masks(widths_ref, first, shape):
    columns = first + lax.broadcasted_iota(jnp.int32, shape, 0)
    masks, low = [], jnp.int32(0)
    for k in range(widths_ref.shape[0]):
        high = low + widths_ref[k]
        masks.append((columns >= low) & (columns < high))
        low = high
    return masks


def keep_of(masks, struct_ref, block):
    keep = jnp.zeros(masks[0].shape, jnp.int32)
    for k, mask in enumerate(masks):
        keep = keep + jnp.where(mask, struct_ref[k, block], 0)
    return keep.astype(jnp.float32)


def kernel(struct_hbm, widths_hbm, p_hbm, a_hbm, o_ref, struct_ref, widths_ref, own, abuf, pbuf, part, crecv, xrecv, frecv,
           in_sem, pair_s, pair_r, up_s, up_r, dn_s, dn_r, late_s, late_r, core_s, core_r, x_s, x_r, f_s, f_r):
    row = lax.axis_index("prow")
    col = lax.axis_index("pcol")
    nprow, npcol = lax.axis_size("prow"), lax.axis_size("pcol")
    yh, z = row // NZ, row % NZ
    yl, x, k = col // (NX * NK), (col // NK) % NX, col % NK

    def dev(yh=yh, z=z, yl=yl, x=x, k=k):
        return (yh * NZ + z, (yl * NX + x) * NK + k)

    def z_at(step):
        return lax.rem(z + step + NZ, NZ)

    loads = [pltpu.make_async_copy(src, dst, in_sem.at[i]) for i, (src, dst) in enumerate(
        [(struct_hbm, struct_ref), (widths_hbm, widths_ref), (p_hbm, own), (a_hbm, abuf)])]
    for load in loads:
        load.start()
    up_dev, dn_dev = dev(z=z_at(1)), dev(z=z_at(-1))
    pair_dev, core_dev = dev(yh=1 - yh), dev(k=1 - k)
    partners = [up_dev, dn_dev, pair_dev] + [(row, lax.rem(col + d, npcol)) for d in range(1, npcol)]
    barrier = pltpu.get_barrier_semaphore()
    for d in partners:
        pl.semaphore_signal(barrier, inc=1, device_id=d, device_id_type=MESH)
    for load in loads[:3]:
        load.wait()
    masks = supernode_masks(widths_ref, row * 48, (48, 256))
    for b in range(6):
        keep = keep_of(masks, struct_ref, b * npcol + col)
        pbuf[z, yh, b] = (own[b].astype(jnp.float32) * keep).astype(jnp.bfloat16)
    pl.semaphore_wait(barrier, len(partners))

    def remote(src, dst, send, recv, device):
        return pltpu.make_async_remote_copy(
            src_ref=src, dst_ref=dst, send_sem=send, recv_sem=recv, device_id=device, device_id_type=MESH)

    def piece(zz, y, second):
        return pbuf.at[zz, y, pl.ds(3 if second else 0, 3)]

    def ring(sems, device):
        def message(s, h, zz):
            ref = piece(zz, 1 - yh if h == 2 else yh, h > 0)
            return remote(ref, ref, sems[0].at[s, h], sems[1].at[s, h], device)
        return message

    up, dn = ring((up_s, up_r), up_dev), ring((dn_s, dn_r), dn_dev)

    def pair(y):
        return remote(piece(z, y, True), piece(z, y, True), pair_s, pair_r, pair_dev)

    def late(t, zz, y):
        return remote(piece(zz, y, False), piece(zz, y, False), late_s.at[t], late_r.at[t], pair_dev)

    def products(zs):
        n = len(zs)
        for a in range(3):
            total = None
            for b in range(6):
                rows = [pbuf[zz, :, b].reshape(96, 256) for zz in zs]
                lhs = rows[0] if n == 1 else jnp.concatenate(rows, axis=0)
                term = lax.dot_general(lhs, abuf[a, b], (((1,), (1,)), ((), ())), preferred_element_type=jnp.float32)
                total = term if total is None else total + term
            for i, zz in enumerate(zs):
                got = total[96 * i:96 * i + 96].reshape(4, 24, 256)
                if a == 0:
                    part[zz, 0, :, :, 0:256] = got
                elif a == 1:
                    part[zz, 0, :, :, 256:384] = got[:, :, 0:128]
                    part[zz, 1, :, :, 0:128] = got[:, :, 128:256]
                else:
                    part[zz, 1, :, :, 128:384] = got

    def core(t, zz):
        return remote(part.at[zz, 1 - k], crecv.at[zz], core_s.at[t], core_r.at[t], core_dev)

    def xcopy(t, zz, d):
        to = lax.rem(x + d, NX)
        return remote(part.at[zz, k, to], xrecv.at[zz, d - 1], x_s.at[t, d - 1], x_r.at[t, d - 1], dev(x=to))

    def owned_here(zz):
        return (zz // 4 == x) & (x // 2 == yl) & ((zz // 2) % 2 == k)

    def fcopy(t, zz):
        h, rh = zz % 2, x % 2
        return remote(part.at[zz, k, x], frecv.at[h, rh, yl, k], f_s.at[t], f_r.at[h, rh, yl, k],
                      dev(x=zz // 4, yl=x // 2, k=(zz // 2) % 2))

    def stage_c(t, zz):
        core(t, zz).wait_recv()
        part[zz, k] = part[zz, k] + crecv[zz]
        for d in (2, 1, 3):
            xcopy(t, zz, d).start()

    def stage_s(t, zz):
        for d in (2, 1, 3):
            xcopy(t, zz, d).wait_recv()
        part[zz, k, x] = part[zz, k, x] + xrecv[zz, 0] + xrecv[zz, 1] + xrecv[zz, 2]

        @pl.when(owned_here(zz))
        def _():
            frecv[zz % 2, x % 2, yl, k] = part[zz, k, x]

        @pl.when(jnp.logical_not(owned_here(zz)))
        def _():
            fcopy(t, zz).start()

    def items(s):
        if isinstance(s, int):
            if s == 0:
                return [(0, z)]
            if s == 8:
                return [(15, z_at(8))]
        return [(2 * s - 1, z_at(-s)), (2 * s, z_at(s))]

    def run(stage, s):
        if isinstance(s, int):
            for t, zz in items(s) if s >= 0 else []:
                stage(t, zz)
            return
        for t, zz in items(s):
            @pl.when(t >= 0)
            def _(t=t, zz=zz):
                stage(t, lax.rem(zz + NZ, NZ))

    def multiply(s):
        for t, zz in items(s):
            late(t, zz, 1 - yh).wait_recv()
        products([zz for _, zz in items(s)])
        for t, zz in items(s):
            core(t, zz).start()

    def when(s, do):
        if isinstance(s, int):
            if s < 7:
                do()
        else:
            pl.when(s < 7)(do)

    def step(s):
        last = isinstance(s, int) and s == 8
        below, above = z_at(-s), z_at(s)
        up(s, 0, below).wait_recv()
        if not last:
            up(s + 1, 0, below).start()
            dn(s, 0, above).wait_recv()
            when(s, dn(s + 1, 0, above).start)
        for t, zz in items(s):
            late(t, zz, yh).start()
        if not (isinstance(s, int) and s < 2):
            multiply(s - 2)
        if not last:
            up(s, 1, below).wait_recv()
            when(s, up(s + 1, 1, below).start)
        dn(s, 1, above).wait_recv()
        if not last:
            dn(s + 1, 1, above).start()
        run(stage_c, s - 3)
        up(s, 2, below).wait_recv()
        if not last:
            up(s + 1, 2, below).start()
            dn(s, 2, above).wait_recv()
            when(s, dn(s + 1, 2, above).start)
        run(stage_s, s - 5)

    for h in range(2):
        up(1, h, z).start()
        dn(1, h, z).start()
        if h == 0:
            pair(yh).start()
    late(0, z, yh).start()
    loads[3].wait()
    pair(1 - yh).wait_recv()
    up(1, 2, z).start()
    dn(1, 2, z).start()
    step(1)
    step(2)

    @pl.loop(3, 8)
    def _(s):
        step(s)

    step(8)
    multiply(7)
    run(stage_c, 6)
    run(stage_s, 4)
    multiply(8)
    run(stage_c, 7)
    run(stage_s, 5)
    run(stage_c, 8)
    run(stage_s, 6)
    run(stage_s, 7)
    run(stage_s, 8)

    masks = supernode_masks(widths_ref, col * 96, (96, 256))
    keeps = [keep_of(masks, struct_ref, a * nprow + row) for a in range(3)]
    for h in range(2):
        zz = 4 * x + 2 * k + h
        halves = []
        for rh in range(2):
            for ys in range(2):
                for ks in range(2):
                    here = (x == 2 * yl + rh) & (ys == yl) & (ks == k)

                    @pl.when(jnp.logical_not(here))
                    def _(rh=rh, ys=ys, ks=ks):
                        remote(frecv.at[h, rh, ys, ks], frecv.at[h, rh, ys, ks], f_s.at[0], f_r.at[h, rh, ys, ks],
                               core_dev).wait_recv()
        halves = [jnp.concatenate([frecv[h, rh, 0, ks] + frecv[h, rh, 1, ks] for rh in range(2)], axis=0) for ks in range(2)]
        lanes = [halves[0][:, 0:256], jnp.concatenate([halves[0][:, 256:384], halves[1][:, 0:128]], axis=1),
                 halves[1][:, 128:384]]
        for a in range(3):
            o_ref[a, 48 * h:48 * h + 48, :] = (-(lanes[a] * keeps[a][48 * h:48 * h + 48])).astype(jnp.bfloat16)

    pair(yh).wait_send()

    @pl.loop(1, 8)
    def _(s):
        for h in range(3):
            up(s, h, z).wait_send()
            dn(s, h, z).wait_send()

    up(8, 0, z).wait_send()
    up(8, 2, z).wait_send()
    dn(8, 1, z).wait_send()

    @pl.loop(0, 16)
    def _(t):
        s = (t + 1) // 2
        zz = lax.rem(z + jnp.where(t % 2 == 1, -s, s) + NZ, NZ)
        late(t, zz, yh).wait_send()
        core(t, zz).wait_send()
        for d in (1, 2, 3):
            xcopy(t, zz, d).wait_send()

        @pl.when(jnp.logical_not(owned_here(zz)))
        def _():
            fcopy(t, zz).wait_send()


def body(ainv, panel, structure, widths):
    a = ainv[:, 0, :, :, 0, :].transpose(0, 2, 1, 3)
    p = panel[:, 0].transpose(0, 2, 1)
    dma, vmem = pltpu.SemaphoreType.DMA, pltpu.VMEM
    f32, bf16 = jnp.float32, jnp.bfloat16
    out = pl.pallas_call(
        kernel,
        out_shape=jax.ShapeDtypeStruct((3, 96, 256), bf16),
        in_specs=[pl.BlockSpec(memory_space=pl.ANY)] * 4,
        out_specs=pl.BlockSpec(memory_space=vmem),
        scratch_shapes=[
            pltpu.SMEM((4, 96), jnp.int32), pltpu.SMEM((4,), jnp.int32), vmem((6, 48, 256), bf16),
            vmem((3, 6, 256, 256), bf16),
            vmem((NZ, NY, 6, 48, 256), bf16),
            vmem((NZ, 2, 4, 24, 384), f32),
            vmem((NZ, 4, 24, 384), f32),
            vmem((NZ, 3, 24, 384), f32),
            vmem((2, 2, 2, 2, 24, 384), f32),
            dma((4,)), dma, dma, dma((9, 3)), dma((9, 3)), dma((9, 3)), dma((9, 3)),
            dma((16,)), dma((16,)), dma((16,)), dma((16,)), dma((16, 3)), dma((16, 3)),
            dma((16,)), dma((2, 2, 2, 2)),
        ],
        compiler_params=pltpu.CompilerParams(
            collective_id=0, has_side_effects=True, vmem_limit_bytes=60 << 20),
        name="gather_multiply_scatter",
    )(structure, widths, p, a)
    return out.transpose(0, 2, 1)[:, None]


def solution(mesh):
    in_specs = (P(None, "prow", None, None, "pcol", None), P(None, "pcol", None, "prow"), P(), P())
    out_specs = P(None, "prow", None, "pcol")
    return jax.shard_map(body, mesh=mesh, in_specs=in_specs, out_specs=out_specs, check_vma=False)
```

```python
import jax
import jax.numpy as jnp
from jax import lax
from jax.experimental import pallas as pl
from jax.experimental.pallas import tpu as pltpu
from jax.sharding import PartitionSpec as P

MESH = pl.DeviceIdType.MESH
SUB = 1
NZ, NY, NX, NK = 16, 2, 4, 2


def supernode_masks(widths_ref, first, shape):
    columns = first + lax.broadcasted_iota(jnp.int32, shape, 0)
    masks, low = [], jnp.int32(0)
    for k in range(widths_ref.shape[0]):
        high = low + widths_ref[k]
        masks.append((columns >= low) & (columns < high))
        low = high
    return masks


def keep_of(masks, struct_ref, block):
    keep = jnp.zeros(masks[0].shape, jnp.int32)
    for k, mask in enumerate(masks):
        keep = keep + jnp.where(mask, struct_ref[k, block], 0)
    return keep.astype(jnp.float32)


def kernel(struct_hbm, widths_hbm, p_hbm, a_hbm, o_ref, struct_ref, widths_ref, own, abuf, pbuf, part, crecv, xrecv, frecv,
           in_sem, pair_s, pair_r, up_s, up_r, dn_s, dn_r, late_s, late_r, core_s, core_r, x_s, x_r, f_s, f_r):
    row = lax.axis_index("prow")
    col = lax.axis_index("pcol")
    nprow, npcol = lax.axis_size("prow"), lax.axis_size("pcol")
    yh, z = row // NZ, row % NZ
    yl, x, k = col // (NX * NK), (col // NK) % NX, col % NK

    def dev(yh=yh, z=z, yl=yl, x=x, k=k):
        return (yh * NZ + z, (yl * NX + x) * NK + k)

    def z_at(step):
        return lax.rem(z + step + NZ, NZ)

    loads = [pltpu.make_async_copy(src, dst, in_sem.at[i]) for i, (src, dst) in enumerate(
        [(struct_hbm, struct_ref), (widths_hbm, widths_ref), (p_hbm, own), (a_hbm, abuf)])]
    for load in loads:
        load.start()
    up_dev, dn_dev = dev(z=z_at(1)), dev(z=z_at(-1))
    pair_dev, core_dev = dev(yh=1 - yh), dev(k=1 - k)
    over_dev, under_dev = dev(yh=1 - yh, z=z_at(1)), dev(yh=1 - yh, z=z_at(-1))
    partners = [up_dev, dn_dev, pair_dev, over_dev, under_dev] + [(row, lax.rem(col + d, npcol)) for d in range(1, npcol)]
    barrier = pltpu.get_barrier_semaphore()
    for d in partners:
        pl.semaphore_signal(barrier, inc=1, device_id=d, device_id_type=MESH)
    for load in loads[:3]:
        load.wait()
    masks = supernode_masks(widths_ref, row * 48, (48, 256))
    for b in range(6):
        keep = keep_of(masks, struct_ref, b * npcol + col)
        pbuf[z, yh, b] = (own[b].astype(jnp.float32) * keep).astype(jnp.bfloat16)
    pl.semaphore_wait(barrier, len(partners))

    def remote(src, dst, send, recv, device):
        return pltpu.make_async_remote_copy(
            src_ref=src, dst_ref=dst, send_sem=send, recv_sem=recv, device_id=device, device_id_type=MESH)

    def piece(zz, y, second):
        return pbuf.at[zz, y, pl.ds(3 if second else 0, 3)]

    def ring(sems, device):
        def message(s, h, zz, i):
            first, n = (3 if h > 0 else 0) + i * (3 // SUB), 3 // SUB
            ref = pbuf.at[zz, 1 - yh if h == 2 else yh, pl.ds(first, n)]
            return remote(ref, ref, sems[0].at[s, h, i], sems[1].at[s, h, i], device)
        return message

    up, dn = ring((up_s, up_r), up_dev), ring((dn_s, dn_r), dn_dev)

    def pair(y):
        return remote(piece(z, y, True), piece(z, y, True), pair_s, pair_r, pair_dev)

    def late(t, zz, y):
        return remote(piece(zz, y, False), piece(zz, y, False), late_s.at[t], late_r.at[t], pair_dev)

    def last_late():
        return remote(piece(z_at(-7), yh, False), piece(z_at(-7), yh, False), late_s.at[15], late_r.at[15], over_dev)

    def products(zs, which):
        n = len(zs)
        for a in which:
            total = None
            for b in range(6):
                rows = [pbuf[zz, :, b].reshape(96, 256) for zz in zs]
                lhs = rows[0] if n == 1 else jnp.concatenate(rows, axis=0)
                term = lax.dot_general(lhs, abuf[a, b], (((1,), (1,)), ((), ())), preferred_element_type=jnp.float32)
                total = term if total is None else total + term
            for i, zz in enumerate(zs):
                got = total[96 * i:96 * i + 96].reshape(4, 24, 256)
                if a == 0:
                    part[zz, 0, :, :, 0:256] = got
                elif a == 1:
                    part[zz, 0, :, :, 256:384] = got[:, :, 0:128]
                    part[zz, 1, :, :, 0:128] = got[:, :, 128:256]
                else:
                    part[zz, 1, :, :, 128:384] = got

    def core(t, zz):
        return remote(part.at[zz, 1 - k], crecv.at[zz], core_s.at[t], core_r.at[t], core_dev)

    def xcopy(t, zz, d):
        to = lax.rem(x + d, NX)
        return remote(part.at[zz, k, to], xrecv.at[zz, d - 1], x_s.at[t, d - 1], x_r.at[t, d - 1], dev(x=to))

    def owned_here(zz):
        return (zz // 4 == x) & (x // 2 == yl) & ((zz // 2) % 2 == k)

    def fcopy(t, zz):
        h, rh = zz % 2, x % 2
        return remote(part.at[zz, k, x], frecv.at[h, rh, yl, k], f_s.at[t], f_r.at[h, rh, yl, k],
                      dev(x=zz // 4, yl=x // 2, k=(zz // 2) % 2))

    def stage_c(t, zz):
        core(t, zz).wait_recv()
        part[zz, k] = part[zz, k] + crecv[zz]
        for d in (2, 1, 3):
            xcopy(t, zz, d).start()

    def stage_s(t, zz):
        for d in (2, 1, 3):
            xcopy(t, zz, d).wait_recv()
        part[zz, k, x] = part[zz, k, x] + xrecv[zz, 0] + xrecv[zz, 1] + xrecv[zz, 2]

        @pl.when(owned_here(zz))
        def _():
            frecv[zz % 2, x % 2, yl, k] = part[zz, k, x]

        @pl.when(jnp.logical_not(owned_here(zz)))
        def _():
            fcopy(t, zz).start()

    def items(s):
        if isinstance(s, int):
            if s == 0:
                return [(0, z)]
            if s == 8:
                return [(15, z_at(8))]
        return [(2 * s - 1, z_at(-s)), (2 * s, z_at(s))]

    def run(stage, s):
        if isinstance(s, int):
            for t, zz in items(s) if s >= 0 else []:
                stage(t, zz)
            return
        for t, zz in items(s):
            @pl.when(t >= 0)
            def _(t=t, zz=zz):
                stage(t, lax.rem(zz + NZ, NZ))

    def when(s, do):
        if isinstance(s, int):
            if s < 7:
                do()
        else:
            pl.when(s < 7)(do)

    def pass_both(s, h, up_on, dn_on):
        below, above = z_at(-s), z_at(s)
        for i in range(SUB):
            up(s, h, below, i).wait_recv()
            if up_on:
                up(s + 1, h, below, i).start()
            else:
                when(s, up(s + 1, h, below, i).start)
            dn(s, h, above, i).wait_recv()
            if dn_on:
                dn(s + 1, h, above, i).start()
            else:
                when(s, dn(s + 1, h, above, i).start)

    def multiply(s):
        for t, zz in items(s):
            late(t, zz, 1 - yh).wait_recv()
        products([zz for _, zz in items(s)], range(3))
        for t, zz in items(s):
            core(t, zz).start()

    def step(s):
        pass_both(s, 0, True, False)
        if not isinstance(s, int):
            pl.when(s == 7)(last_late().start)
        for t, zz in items(s):
            late(t, zz, yh).start()
        run(stage_c, s - 2)
        pass_both(s, 1, False, True)
        pass_both(s, 2, True, False)
        multiply(s - 1)
        run(stage_s, s - 3)

    for h in range(2):
        for i in range(SUB):
            up(1, h, z, i).start()
            dn(1, h, z, i).start()
        if h == 0:
            pair(yh).start()
    late(0, z, yh).start()
    pair(1 - yh).wait_recv()
    for i in range(SUB):
        up(1, 2, z, i).start()
        dn(1, 2, z, i).start()
    loads[3].wait()
    step(1)

    @pl.loop(2, 8)
    def _(s):
        step(s)

    for i in range(SUB):
        up(8, 0, z_at(8), i).wait_recv()
    run(stage_c, 6)
    for i in range(SUB):
        dn(8, 1, z_at(8), i).wait_recv()
    for i in range(SUB):
        up(8, 2, z_at(8), i).wait_recv()
    multiply(7)
    run(stage_s, 5)
    multiply(8)
    run(stage_c, 7)
    run(stage_c, 8)
    run(stage_s, 6)
    run(stage_s, 7)
    run(stage_s, 8)

    masks = supernode_masks(widths_ref, col * 96, (96, 256))
    keeps = [keep_of(masks, struct_ref, a * nprow + row) for a in range(3)]
    for h in range(2):
        zz = 4 * x + 2 * k + h
        halves = []
        for rh in range(2):
            for ys in range(2):
                for ks in range(2):
                    here = (x == 2 * yl + rh) & (ys == yl) & (ks == k)

                    @pl.when(jnp.logical_not(here))
                    def _(rh=rh, ys=ys, ks=ks):
                        remote(frecv.at[h, rh, ys, ks], frecv.at[h, rh, ys, ks], f_s.at[0], f_r.at[h, rh, ys, ks],
                               core_dev).wait_recv()
        halves = [jnp.concatenate([frecv[h, rh, 0, ks] + frecv[h, rh, 1, ks] for rh in range(2)], axis=0) for ks in range(2)]
        lanes = [halves[0][:, 0:256], jnp.concatenate([halves[0][:, 256:384], halves[1][:, 0:128]], axis=1),
                 halves[1][:, 128:384]]
        for a in range(3):
            o_ref[a, 48 * h:48 * h + 48, :] = (-(lanes[a] * keeps[a][48 * h:48 * h + 48])).astype(jnp.bfloat16)

    pair(yh).wait_send()

    @pl.loop(1, 8)
    def _(s):
        for h in range(3):
            for i in range(SUB):
                up(s, h, z, i).wait_send()
                dn(s, h, z, i).wait_send()

    @pl.loop(0, 15)
    def _(t):
        late(t, z, yh).wait_send()

    last_late().wait_send()
    for i in range(SUB):
        up(8, 0, z, i).wait_send()
        up(8, 2, z, i).wait_send()
        dn(8, 1, z, i).wait_send()

    @pl.loop(0, 16)
    def _(t):
        s = (t + 1) // 2
        zz = lax.rem(z + jnp.where(t % 2 == 1, -s, s) + NZ, NZ)
        core(t, zz).wait_send()
        for d in (1, 2, 3):
            xcopy(t, zz, d).wait_send()

        @pl.when(jnp.logical_not(owned_here(zz)))
        def _():
            fcopy(t, zz).wait_send()


def body(ainv, panel, structure, widths):
    a = ainv[:, 0, :, :, 0, :].transpose(0, 2, 1, 3)
    p = panel[:, 0].transpose(0, 2, 1)
    dma, vmem = pltpu.SemaphoreType.DMA, pltpu.VMEM
    f32, bf16 = jnp.float32, jnp.bfloat16
    out = pl.pallas_call(
        kernel,
        out_shape=jax.ShapeDtypeStruct((3, 96, 256), bf16),
        in_specs=[pl.BlockSpec(memory_space=pl.ANY)] * 4,
        out_specs=pl.BlockSpec(memory_space=vmem),
        scratch_shapes=[
            pltpu.SMEM((4, 96), jnp.int32), pltpu.SMEM((4,), jnp.int32), vmem((6, 48, 256), bf16),
            vmem((3, 6, 256, 256), bf16),
            vmem((NZ, NY, 6, 48, 256), bf16),
            vmem((NZ, 2, 4, 24, 384), f32),
            vmem((NZ, 4, 24, 384), f32),
            vmem((NZ, 3, 24, 384), f32),
            vmem((2, 2, 2, 2, 24, 384), f32),
            dma((4,)), dma, dma, dma((9, 3, SUB)), dma((9, 3, SUB)), dma((9, 3, SUB)), dma((9, 3, SUB)),
            dma((16,)), dma((16,)), dma((16,)), dma((16,)), dma((16, 3)), dma((16, 3)),
            dma((16,)), dma((2, 2, 2, 2)),
        ],
        compiler_params=pltpu.CompilerParams(
            collective_id=0, has_side_effects=True, vmem_limit_bytes=60 << 20),
        name="gather_multiply_scatter",
    )(structure, widths, p, a)
    return out.transpose(0, 2, 1)[:, None]


def solution(mesh):
    in_specs = (P(None, "prow", None, None, "pcol", None), P(None, "pcol", None, "prow"), P(), P())
    out_specs = P(None, "prow", None, "pcol")
    return jax.shard_map(body, mesh=mesh, in_specs=in_specs, out_specs=out_specs, check_vma=False)
```

```python
import jax
import jax.numpy as jnp
from jax import lax
from jax.experimental import pallas as pl
from jax.experimental.pallas import tpu as pltpu
from jax.sharding import PartitionSpec as P

MESH = pl.DeviceIdType.MESH
NZ, NY, NX, NK = 16, 2, 4, 2


def supernode_masks(widths_ref, first, shape):
    columns = first + lax.broadcasted_iota(jnp.int32, shape, 0)
    masks, low = [], jnp.int32(0)
    for k in range(widths_ref.shape[0]):
        high = low + widths_ref[k]
        masks.append((columns >= low) & (columns < high))
        low = high
    return masks


def keep_of(masks, struct_ref, block):
    keep = jnp.zeros(masks[0].shape, jnp.int32)
    for k, mask in enumerate(masks):
        keep = keep + jnp.where(mask, struct_ref[k, block], 0)
    return keep.astype(jnp.float32)


def kernel(struct_hbm, widths_hbm, p_hbm, a_hbm, o_ref, struct_ref, widths_ref, own, abuf, pbuf, part, crecv, xrecv, frecv,
           in_sem, pair_s, pair_r, up_s, up_r, dn_s, dn_r, late_s, late_r, core_s, core_r, x_s, x_r, f_s, f_r):
    row = lax.axis_index("prow")
    col = lax.axis_index("pcol")
    nprow, npcol = lax.axis_size("prow"), lax.axis_size("pcol")
    yh, z = row // NZ, row % NZ
    yl, x, k = col // (NX * NK), (col // NK) % NX, col % NK

    def dev(yh=yh, z=z, yl=yl, x=x, k=k):
        return (yh * NZ + z, (yl * NX + x) * NK + k)

    def z_at(step):
        return lax.rem(z + step + NZ, NZ)

    loads = [pltpu.make_async_copy(src, dst, in_sem.at[i]) for i, (src, dst) in enumerate(
        [(struct_hbm, struct_ref), (widths_hbm, widths_ref), (p_hbm, own), (a_hbm, abuf)])]
    for load in loads:
        load.start()
    up_dev, dn_dev = dev(z=z_at(1)), dev(z=z_at(-1))
    pair_dev, core_dev = dev(yh=1 - yh), dev(k=1 - k)
    over_dev, under_dev = dev(yh=1 - yh, z=z_at(1)), dev(yh=1 - yh, z=z_at(-1))
    partners = [up_dev, dn_dev, pair_dev, over_dev, under_dev] + [(row, lax.rem(col + d, npcol)) for d in range(1, npcol)]
    barrier = pltpu.get_barrier_semaphore()
    for d in partners:
        pl.semaphore_signal(barrier, inc=1, device_id=d, device_id_type=MESH)
    for load in loads[:3]:
        load.wait()
    masks = supernode_masks(widths_ref, row * 48, (48, 256))
    for b in range(6):
        keep = keep_of(masks, struct_ref, b * npcol + col)
        pbuf[z, yh, b] = (own[b].astype(jnp.float32) * keep).astype(jnp.bfloat16)
    pl.semaphore_wait(barrier, len(partners))

    def remote(src, dst, send, recv, device):
        return pltpu.make_async_remote_copy(
            src_ref=src, dst_ref=dst, send_sem=send, recv_sem=recv, device_id=device, device_id_type=MESH)

    def piece(zz, y, second):
        return pbuf.at[zz, y, pl.ds(3 if second else 0, 3)]

    def ring(sems, device):
        def message(s, h, zz):
            ref = piece(zz, 1 - yh if h == 2 else yh, h > 0)
            return remote(ref, ref, sems[0].at[s, h], sems[1].at[s, h], device)
        return message

    up, dn = ring((up_s, up_r), up_dev), ring((dn_s, dn_r), dn_dev)

    def pair(y):
        return remote(piece(z, y, True), piece(z, y, True), pair_s, pair_r, pair_dev)

    def late(t, zz, y):
        return remote(piece(zz, y, False), piece(zz, y, False), late_s.at[t], late_r.at[t], pair_dev)

    def last_late():
        return remote(piece(z_at(-7), yh, False), piece(z_at(-7), yh, False), late_s.at[15], late_r.at[15], over_dev)

    def products(zs, which):
        n = len(zs)
        for a in which:
            total = None
            for b in range(6):
                rows = [pbuf[zz, :, b].reshape(96, 256) for zz in zs]
                lhs = rows[0] if n == 1 else jnp.concatenate(rows, axis=0)
                term = lax.dot_general(lhs, abuf[a, b], (((1,), (1,)), ((), ())), preferred_element_type=jnp.float32)
                total = term if total is None else total + term
            for i, zz in enumerate(zs):
                got = total[96 * i:96 * i + 96].reshape(4, 24, 256)
                if a == 0:
                    part[zz, 0, :, :, 0:256] = got
                elif a == 1:
                    part[zz, 0, :, :, 256:384] = got[:, :, 0:128]
                    part[zz, 1, :, :, 0:128] = got[:, :, 128:256]
                else:
                    part[zz, 1, :, :, 128:384] = got

    def core(t, zz):
        return remote(part.at[zz, 1 - k], crecv.at[zz], core_s.at[t], core_r.at[t], core_dev)

    def xcopy(t, zz, d):
        to = lax.rem(x + d, NX)
        return remote(part.at[zz, k, to], xrecv.at[zz, d - 1], x_s.at[t, d - 1], x_r.at[t, d - 1], dev(x=to))

    def owned_here(zz):
        return (zz // 4 == x) & (x // 2 == yl) & ((zz // 2) % 2 == k)

    def fcopy(t, zz):
        h, rh = zz % 2, x % 2
        return remote(part.at[zz, k, x], frecv.at[h, rh, yl, k], f_s.at[t], f_r.at[h, rh, yl, k],
                      dev(x=zz // 4, yl=x // 2, k=(zz // 2) % 2))

    def stage_c(t, zz):
        core(t, zz).wait_recv()
        part[zz, k] = part[zz, k] + crecv[zz]
        for d in (2, 1, 3):
            xcopy(t, zz, d).start()

    def stage_s(t, zz):
        for d in (2, 1, 3):
            xcopy(t, zz, d).wait_recv()
        part[zz, k, x] = part[zz, k, x] + xrecv[zz, 0] + xrecv[zz, 1] + xrecv[zz, 2]

        @pl.when(owned_here(zz))
        def _():
            frecv[zz % 2, x % 2, yl, k] = part[zz, k, x]

        @pl.when(jnp.logical_not(owned_here(zz)))
        def _():
            fcopy(t, zz).start()

    def z_of(t):
        s = (t + 1) // 2
        return lax.rem(z + jnp.where(t % 2 == 1, -s, s) + NZ, NZ)

    def items(s):
        if isinstance(s, int):
            if s == 0:
                return [(0, z)]
            if s == 8:
                return [(15, z_at(8))]
        return [(2 * s - 1, z_at(-s)), (2 * s, z_at(s))]

    def run(stage, s):
        if isinstance(s, int):
            for t, zz in items(s) if s >= 0 else []:
                stage(t, zz)
            return
        for t, zz in items(s):
            @pl.when(t >= 0)
            def _(t=t, zz=zz):
                stage(t, lax.rem(zz + NZ, NZ))

    def when(s, do):
        if isinstance(s, int):
            if s < 7:
                do()
        else:
            pl.when(s < 7)(do)

    def pass_both(s, h, up_on, dn_on):
        below, above = z_at(-s), z_at(s)
        up(s, h, below).wait_recv()
        if up_on:
            up(s + 1, h, below).start()
        else:
            when(s, up(s + 1, h, below).start)
        dn(s, h, above).wait_recv()
        if dn_on:
            dn(s + 1, h, above).start()
        else:
            when(s, dn(s + 1, h, above).start)

    def multiply(*steps):
        pairs = [item for s in steps for item in items(s)]
        for t, zz in pairs:
            late(t, zz, 1 - yh).wait_recv()
        products([zz for _, zz in pairs], range(3))
        for t, zz in pairs:
            core(t, zz).start()

    def step(s):
        pass_both(s, 0, True, False)
        if not isinstance(s, int):
            pl.when(s == 7)(last_late().start)
        for t, zz in items(s):
            late(t, zz, yh).start()
        run(stage_c, s - 2)
        pass_both(s, 1, False, True)
        pass_both(s, 2, True, False)
        multiply(s - 1)
        run(stage_s, s - 3)

    for h in range(2):
        up(1, h, z).start()
        dn(1, h, z).start()
        if h == 0:
            pair(yh).start()
    late(0, z, yh).start()
    pair(1 - yh).wait_recv()
    up(1, 2, z).start()
    dn(1, 2, z).start()
    loads[3].wait()
    step(1)

    @pl.loop(2, 8)
    def _(s):
        step(s)

    up(8, 0, z_at(8)).wait_recv()
    run(stage_c, 6)
    dn(8, 1, z_at(8)).wait_recv()
    up(8, 2, z_at(8)).wait_recv()
    run(stage_s, 5)
    multiply(7, 8)
    run(stage_c, 7)
    run(stage_c, 8)
    run(stage_s, 6)
    pair(yh).wait_send()

    @pl.loop(1, 8)
    def _(s):
        for h in range(3):
            up(s, h, z).wait_send()
            dn(s, h, z).wait_send()

    @pl.loop(0, 15)
    def _(t):
        late(t, z, yh).wait_send()

    last_late().wait_send()
    up(8, 0, z).wait_send()
    up(8, 2, z).wait_send()
    dn(8, 1, z).wait_send()

    @pl.loop(0, 16)
    def _(t):
        core(t, z_of(t)).wait_send()

    run(stage_s, 7)
    run(stage_s, 8)

    @pl.loop(0, 16)
    def _(t):
        for d in (1, 2, 3):
            xcopy(t, z_of(t), d).wait_send()

    masks = supernode_masks(widths_ref, col * 96, (96, 256))
    keeps = [keep_of(masks, struct_ref, a * nprow + row) for a in range(3)]
    for h in range(2):
        zz = 4 * x + 2 * k + h
        halves = []
        for rh in range(2):
            for ys in range(2):
                for ks in range(2):
                    here = (x == 2 * yl + rh) & (ys == yl) & (ks == k)

                    @pl.when(jnp.logical_not(here))
                    def _(rh=rh, ys=ys, ks=ks):
                        remote(frecv.at[h, rh, ys, ks], frecv.at[h, rh, ys, ks], f_s.at[0], f_r.at[h, rh, ys, ks],
                               core_dev).wait_recv()
        halves = [jnp.concatenate([frecv[h, rh, 0, ks] + frecv[h, rh, 1, ks] for rh in range(2)], axis=0) for ks in range(2)]
        lanes = [halves[0][:, 0:256], jnp.concatenate([halves[0][:, 256:384], halves[1][:, 0:128]], axis=1),
                 halves[1][:, 128:384]]
        for a in range(3):
            o_ref[a, 48 * h:48 * h + 48, :] = (-(lanes[a] * keeps[a][48 * h:48 * h + 48])).astype(jnp.bfloat16)

    @pl.loop(0, 16)
    def _(t):
        zz = z_of(t)

        @pl.when(jnp.logical_not(owned_here(zz)))
        def _():
            fcopy(t, zz).wait_send()


def body(ainv, panel, structure, widths):
    a = ainv[:, 0, :, :, 0, :].transpose(0, 2, 1, 3)
    p = panel[:, 0].transpose(0, 2, 1)
    dma, vmem = pltpu.SemaphoreType.DMA, pltpu.VMEM
    f32, bf16 = jnp.float32, jnp.bfloat16
    out = pl.pallas_call(
        kernel,
        out_shape=jax.ShapeDtypeStruct((3, 96, 256), bf16),
        in_specs=[pl.BlockSpec(memory_space=pltpu.HBM)] * 4,
        out_specs=pl.BlockSpec(memory_space=vmem),
        scratch_shapes=[
            pltpu.SMEM((4, 96), jnp.int32), pltpu.SMEM((4,), jnp.int32), vmem((6, 48, 256), bf16),
            vmem((3, 6, 256, 256), bf16),
            vmem((NZ, NY, 6, 48, 256), bf16),
            vmem((NZ, 2, 4, 24, 384), f32),
            vmem((NZ, 4, 24, 384), f32),
            vmem((NZ, 3, 24, 384), f32),
            vmem((2, 2, 2, 2, 24, 384), f32),
            dma((4,)), dma, dma, dma((9, 3)), dma((9, 3)), dma((9, 3)), dma((9, 3)),
            dma((16,)), dma((16,)), dma((16,)), dma((16,)), dma((16, 3)), dma((16, 3)),
            dma((16,)), dma((2, 2, 2, 2)),
        ],
        compiler_params=pltpu.CompilerParams(
            collective_id=0, has_side_effects=True, vmem_limit_bytes=32 << 20),
        name="gather_multiply_scatter",
    )(*(pltpu.with_memory_space_constraint(v, pltpu.HBM) for v in (structure, widths, p, a)))
    return out.transpose(0, 2, 1)[:, None]


def solution(mesh):
    in_specs = (P(None, "prow", None, None, "pcol", None), P(None, "pcol", None, "prow"), P(), P())
    out_specs = P(None, "prow", None, "pcol")
    return jax.shard_map(body, mesh=mesh, in_specs=in_specs, out_specs=out_specs, check_vma=False)
```

```python
import jax
import jax.numpy as jnp
from jax import lax
from jax.experimental import pallas as pl
from jax.experimental.pallas import tpu as pltpu
from jax.sharding import PartitionSpec as P

MESH = pl.DeviceIdType.MESH
NZ, NY, NX, NK = 16, 2, 4, 2


def supernode_masks(widths_ref, first, shape):
    columns = first + lax.broadcasted_iota(jnp.int32, shape, 0)
    masks, low = [], jnp.int32(0)
    for k in range(widths_ref.shape[0]):
        high = low + widths_ref[k]
        masks.append((columns >= low) & (columns < high))
        low = high
    return masks


def keep_of(masks, struct_ref, block):
    keep = jnp.zeros(masks[0].shape, jnp.int32)
    for k, mask in enumerate(masks):
        keep = keep + jnp.where(mask, struct_ref[k, block], 0)
    return keep.astype(jnp.float32)


def kernel(struct_hbm, widths_hbm, p_hbm, a_hbm, o_ref, struct_ref, widths_ref, own, abuf, pbuf, part, crecv, xrecv, frecv,
           in_sem, pair_s, pair_r, up_s, up_r, dn_s, dn_r, late_s, late_r, core_s, core_r, x_s, x_r, f_s, f_r,
           known):
    row = lax.axis_index("prow")
    col = lax.axis_index("pcol")
    nprow, npcol = lax.axis_size("prow"), lax.axis_size("pcol")
    yh, z = row // NZ, row % NZ
    yl, x, k = col // (NX * NK), (col // NK) % NX, col % NK

    def dev(yh=yh, z=z, yl=yl, x=x, k=k):
        return (yh * NZ + z, (yl * NX + x) * NK + k)

    def z_at(step):
        return lax.rem(z + step + NZ, NZ)

    loads = [pltpu.make_async_copy(src, dst, in_sem.at[i]) for i, (src, dst) in enumerate(
        [(struct_hbm, struct_ref), (widths_hbm, widths_ref), (p_hbm, own), (a_hbm, abuf)])]
    for load in loads:
        load.start()
    up_dev, dn_dev = dev(z=z_at(1)), dev(z=z_at(-1))
    pair_dev, core_dev, over_dev = dev(yh=1 - yh), dev(k=1 - k), dev(yh=1 - yh, z=z_at(1))
    y_dev, next_dev = dev(yl=1 - yl), dev(x=lax.rem(x + 1, NX))
    partners = [up_dev, dn_dev, pair_dev, core_dev, y_dev, next_dev, dev(x=lax.rem(x + 3, NX))]
    rounds = [[core_dev, pair_dev], [y_dev], [next_dev]]

    def tell(i):
        for d in rounds[i]:
            pl.semaphore_signal(known.at[i], inc=1, device_id=d, device_id_type=MESH)

    def learn(i):
        pl.semaphore_wait(known.at[i], len(rounds[i]))

    barrier = pltpu.get_barrier_semaphore()
    for d in partners:
        pl.semaphore_signal(barrier, inc=1, device_id=d, device_id_type=MESH)
    for load in loads[:3]:
        load.wait()
    masks = supernode_masks(widths_ref, row * 48, (48, 256))
    for b in range(6):
        keep = keep_of(masks, struct_ref, b * npcol + col)
        pbuf[z, yh, b] = (own[b].astype(jnp.float32) * keep).astype(jnp.bfloat16)
    pl.semaphore_wait(barrier, len(partners))

    def remote(src, dst, send, recv, device):
        return pltpu.make_async_remote_copy(
            src_ref=src, dst_ref=dst, send_sem=send, recv_sem=recv, device_id=device, device_id_type=MESH)

    def piece(zz, y, second):
        return pbuf.at[zz, y, pl.ds(3 if second else 0, 3)]

    def ring(sems, device):
        def message(s, h, zz):
            ref = piece(zz, 1 - yh if h == 2 else yh, h > 0)
            return remote(ref, ref, sems[0].at[s, h], sems[1].at[s, h], device)
        return message

    up, dn = ring((up_s, up_r), up_dev), ring((dn_s, dn_r), dn_dev)

    def pair(y):
        return remote(piece(z, y, True), piece(z, y, True), pair_s, pair_r, pair_dev)

    def late(t, zz, y):
        return remote(piece(zz, y, False), piece(zz, y, False), late_s.at[t], late_r.at[t], pair_dev)

    def last_late():
        return remote(piece(z_at(-7), yh, False), piece(z_at(-7), yh, False), late_s.at[15], late_r.at[15], over_dev)

    def products(zs, which):
        n = len(zs)
        for a in which:
            total = None
            for b in range(6):
                rows = [pbuf[zz, :, b].reshape(96, 256) for zz in zs]
                lhs = rows[0] if n == 1 else jnp.concatenate(rows, axis=0)
                term = lax.dot_general(lhs, abuf[a, b], (((1,), (1,)), ((), ())), preferred_element_type=jnp.float32)
                total = term if total is None else total + term
            for i, zz in enumerate(zs):
                got = total[96 * i:96 * i + 96].reshape(4, 24, 256)
                if a == 0:
                    part[zz, 0, :, :, 0:256] = got
                elif a == 1:
                    part[zz, 0, :, :, 256:384] = got[:, :, 0:128]
                    part[zz, 1, :, :, 0:128] = got[:, :, 128:256]
                else:
                    part[zz, 1, :, :, 128:384] = got

    def core(t, zz):
        return remote(part.at[zz, 1 - k], crecv.at[zz], core_s.at[t], core_r.at[t], core_dev)

    def xcopy(t, zz, d):
        to = lax.rem(x + d, NX)
        return remote(part.at[zz, k, to], xrecv.at[zz, d - 1], x_s.at[t, d - 1], x_r.at[t, d - 1], dev(x=to))

    def owned_here(zz):
        return (zz // 4 == x) & (x // 2 == yl) & ((zz // 2) % 2 == k)

    def fcopy(t, zz):
        h, rh = zz % 2, x % 2
        return remote(part.at[zz, k, x], frecv.at[h, rh, yl, k], f_s.at[t], f_r.at[h, rh, yl, k],
                      dev(x=zz // 4, yl=x // 2, k=(zz // 2) % 2))

    def stage_c(t, zz):
        core(t, zz).wait_recv()
        part[zz, k] = part[zz, k] + crecv[zz]
        for d in (2, 1, 3):
            xcopy(t, zz, d).start()

    def stage_s(t, zz):
        for d in (2, 1, 3):
            xcopy(t, zz, d).wait_recv()
        part[zz, k, x] = part[zz, k, x] + xrecv[zz, 0] + xrecv[zz, 1] + xrecv[zz, 2]

        @pl.when(owned_here(zz))
        def _():
            frecv[zz % 2, x % 2, yl, k] = part[zz, k, x]

        @pl.when(jnp.logical_not(owned_here(zz)))
        def _():
            fcopy(t, zz).start()

    def z_of(t):
        s = (t + 1) // 2
        return lax.rem(z + jnp.where(t % 2 == 1, -s, s) + NZ, NZ)

    def items(s):
        if isinstance(s, int):
            if s == 0:
                return [(0, z)]
            if s == 8:
                return [(15, z_at(8))]
        return [(2 * s - 1, z_at(-s)), (2 * s, z_at(s))]

    def run(stage, s):
        if isinstance(s, int):
            for t, zz in items(s) if s >= 0 else []:
                stage(t, zz)
            return
        for t, zz in items(s):
            @pl.when(t >= 0)
            def _(t=t, zz=zz):
                stage(t, lax.rem(zz + NZ, NZ))

    def when(s, do):
        if isinstance(s, int):
            if s < 7:
                do()
        else:
            pl.when(s < 7)(do)

    def pass_both(s, h, up_on, dn_on):
        below, above = z_at(-s), z_at(s)
        up(s, h, below).wait_recv()
        if up_on:
            up(s + 1, h, below).start()
        else:
            when(s, up(s + 1, h, below).start)
        dn(s, h, above).wait_recv()
        if dn_on:
            dn(s + 1, h, above).start()
        else:
            when(s, dn(s + 1, h, above).start)

    def multiply(*steps):
        pairs = [item for s in steps for item in items(s)]
        for t, zz in pairs:
            late(t, zz, 1 - yh).wait_recv()
        products([zz for _, zz in pairs], range(3))
        for t, zz in pairs:
            core(t, zz).start()

    def step(s):
        pass_both(s, 0, True, False)
        if not isinstance(s, int):
            pl.when(s == 7)(last_late().start)
        for t, zz in items(s):
            late(t, zz, yh).start()
        run(stage_c, s - 2)
        pass_both(s, 1, False, True)
        pass_both(s, 2, True, False)
        multiply(s - 1)
        run(stage_s, s - 3)

    for h in range(2):
        up(1, h, z).start()
        dn(1, h, z).start()
        if h == 0:
            pair(yh).start()
    late(0, z, yh).start()
    tell(0)
    pair(1 - yh).wait_recv()
    up(1, 2, z).start()
    dn(1, 2, z).start()
    loads[3].wait()
    learn(0)
    tell(1)
    learn(1)
    tell(2)
    step(1)
    learn(2)

    @pl.loop(2, 8)
    def _(s):
        step(s)

    up(8, 0, z_at(8)).wait_recv()
    run(stage_c, 6)
    dn(8, 1, z_at(8)).wait_recv()
    up(8, 2, z_at(8)).wait_recv()
    run(stage_s, 5)
    multiply(7, 8)
    run(stage_c, 7)
    run(stage_c, 8)
    run(stage_s, 6)
    pair(yh).wait_send()

    @pl.loop(1, 8)
    def _(s):
        for h in range(3):
            up(s, h, z).wait_send()
            dn(s, h, z).wait_send()

    @pl.loop(0, 15)
    def _(t):
        late(t, z, yh).wait_send()

    last_late().wait_send()
    up(8, 0, z).wait_send()
    up(8, 2, z).wait_send()
    dn(8, 1, z).wait_send()

    @pl.loop(0, 16)
    def _(t):
        core(t, z_of(t)).wait_send()

    run(stage_s, 7)
    run(stage_s, 8)

    @pl.loop(0, 16)
    def _(t):
        for d in (1, 2, 3):
            xcopy(t, z_of(t), d).wait_send()

    masks = supernode_masks(widths_ref, col * 96, (96, 256))
    keeps = [keep_of(masks, struct_ref, a * nprow + row) for a in range(3)]
    for h in range(2):
        zz = 4 * x + 2 * k + h
        halves = []
        for rh in range(2):
            for ys in range(2):
                for ks in range(2):
                    here = (x == 2 * yl + rh) & (ys == yl) & (ks == k)

                    @pl.when(jnp.logical_not(here))
                    def _(rh=rh, ys=ys, ks=ks):
                        remote(frecv.at[h, rh, ys, ks], frecv.at[h, rh, ys, ks], f_s.at[0], f_r.at[h, rh, ys, ks],
                               core_dev).wait_recv()
        halves = [jnp.concatenate([frecv[h, rh, 0, ks] + frecv[h, rh, 1, ks] for rh in range(2)], axis=0) for ks in range(2)]
        lanes = [halves[0][:, 0:256], jnp.concatenate([halves[0][:, 256:384], halves[1][:, 0:128]], axis=1),
                 halves[1][:, 128:384]]
        for a in range(3):
            o_ref[a, 48 * h:48 * h + 48, :] = (-(lanes[a] * keeps[a][48 * h:48 * h + 48])).astype(jnp.bfloat16)

    @pl.loop(0, 16)
    def _(t):
        zz = z_of(t)

        @pl.when(jnp.logical_not(owned_here(zz)))
        def _():
            fcopy(t, zz).wait_send()


def body(ainv, panel, structure, widths):
    a = ainv[:, 0, :, :, 0, :].transpose(0, 2, 1, 3)
    p = panel[:, 0].transpose(0, 2, 1)
    dma, vmem = pltpu.SemaphoreType.DMA, pltpu.VMEM
    f32, bf16 = jnp.float32, jnp.bfloat16
    out = pl.pallas_call(
        kernel,
        out_shape=jax.ShapeDtypeStruct((3, 96, 256), bf16),
        in_specs=[pl.BlockSpec(memory_space=pltpu.HBM)] * 4,
        out_specs=pl.BlockSpec(memory_space=vmem),
        scratch_shapes=[
            pltpu.SMEM((4, 96), jnp.int32), pltpu.SMEM((4,), jnp.int32), vmem((6, 48, 256), bf16),
            vmem((3, 6, 256, 256), bf16),
            vmem((NZ, NY, 6, 48, 256), bf16),
            vmem((NZ, 2, 4, 24, 384), f32),
            vmem((NZ, 4, 24, 384), f32),
            vmem((NZ, 3, 24, 384), f32),
            vmem((2, 2, 2, 2, 24, 384), f32),
            dma((4,)), dma, dma, dma((9, 3)), dma((9, 3)), dma((9, 3)), dma((9, 3)),
            dma((16,)), dma((16,)), dma((16,)), dma((16,)), dma((16, 3)), dma((16, 3)),
            dma((16,)), dma((2, 2, 2, 2)), pltpu.SemaphoreType.REGULAR((3,)),
        ],
        compiler_params=pltpu.CompilerParams(
            collective_id=0, has_side_effects=True, vmem_limit_bytes=32 << 20),
        name="gather_multiply_scatter",
    )(*(pltpu.with_memory_space_constraint(v, pltpu.HBM) for v in (structure, widths, p, a)))
    return out.transpose(0, 2, 1)[:, None]


def solution(mesh):
    in_specs = (P(None, "prow", None, None, "pcol", None), P(None, "pcol", None, "prow"), P(), P())
    out_specs = P(None, "prow", None, "pcol")
    return jax.shard_map(body, mesh=mesh, in_specs=in_specs, out_specs=out_specs, check_vma=False)
```

```python
import jax
import jax.numpy as jnp
from jax import lax
from jax.experimental import pallas as pl
from jax.experimental.pallas import tpu as pltpu
from jax.sharding import PartitionSpec as P

MESH = pl.DeviceIdType.MESH
NZ, NY, NX, NK = 16, 2, 4, 2


def supernode_masks(widths_ref, first, shape):
    columns = first + lax.broadcasted_iota(jnp.int32, shape, 0)
    masks, low = [], jnp.int32(0)
    for k in range(widths_ref.shape[0]):
        high = low + widths_ref[k]
        masks.append((columns >= low) & (columns < high))
        low = high
    return masks


def keep_of(masks, struct_ref, block):
    keep = jnp.zeros(masks[0].shape, jnp.int32)
    for k, mask in enumerate(masks):
        keep = keep + jnp.where(mask, struct_ref[k, block], 0)
    return keep.astype(jnp.float32)


def kernel(struct_hbm, widths_hbm, p_hbm, a_hbm, o_ref, struct_ref, widths_ref, own, abuf, pbuf, part, crecv, xrecv, frecv,
           in_sem, pair_s, pair_r, up_s, up_r, dn_s, dn_r, late_s, late_r, core_s, core_r, x_s, x_r, f_s, f_r,
           known):
    row = lax.axis_index("prow")
    col = lax.axis_index("pcol")
    nprow, npcol = lax.axis_size("prow"), lax.axis_size("pcol")
    yh, z = row // NZ, row % NZ
    yl, x, k = col // (NX * NK), (col // NK) % NX, col % NK

    def dev(yh=yh, z=z, yl=yl, x=x, k=k):
        return (yh * NZ + z, (yl * NX + x) * NK + k)

    def z_at(step):
        return lax.rem(z + step + NZ, NZ)

    loads = [pltpu.make_async_copy(src, dst, in_sem.at[i]) for i, (src, dst) in enumerate(
        [(struct_hbm, struct_ref), (widths_hbm, widths_ref), (p_hbm, own), (a_hbm, abuf)])]
    for load in loads:
        load.start()
    up_dev, dn_dev = dev(z=z_at(1)), dev(z=z_at(-1))
    pair_dev, core_dev, under_dev = dev(yh=1 - yh), dev(k=1 - k), dev(yh=1 - yh, z=z_at(-1))
    y_dev, next_dev = dev(yl=1 - yl), dev(x=lax.rem(x + 1, NX))
    partners = [up_dev, dn_dev, pair_dev, core_dev, y_dev, next_dev, dev(x=lax.rem(x + 3, NX))]
    rounds = [[core_dev, pair_dev], [y_dev], [next_dev]]

    def tell(i):
        for d in rounds[i]:
            pl.semaphore_signal(known.at[i], inc=1, device_id=d, device_id_type=MESH)

    def learn(i):
        pl.semaphore_wait(known.at[i], len(rounds[i]))

    barrier = pltpu.get_barrier_semaphore()
    for d in partners:
        pl.semaphore_signal(barrier, inc=1, device_id=d, device_id_type=MESH)
    for load in loads[:3]:
        load.wait()
    masks = supernode_masks(widths_ref, row * 48, (48, 256))
    for b in range(6):
        keep = keep_of(masks, struct_ref, b * npcol + col)
        pbuf[z, yh, b] = (own[b].astype(jnp.float32) * keep).astype(jnp.bfloat16)
    pl.semaphore_wait(barrier, len(partners))

    def remote(src, dst, send, recv, device):
        return pltpu.make_async_remote_copy(
            src_ref=src, dst_ref=dst, send_sem=send, recv_sem=recv, device_id=device, device_id_type=MESH)

    def piece(zz, y, second):
        return pbuf.at[zz, y, pl.ds(3 if second else 0, 3)]

    def ring(sems, device):
        def message(s, h, zz):
            ref = piece(zz, 1 - yh if h == 2 else yh, h > 0)
            return remote(ref, ref, sems[0].at[s, h], sems[1].at[s, h], device)
        return message

    up, dn = ring((up_s, up_r), up_dev), ring((dn_s, dn_r), dn_dev)

    def pair(y):
        return remote(piece(z, y, True), piece(z, y, True), pair_s, pair_r, pair_dev)

    def late(t, zz, y):
        return remote(piece(zz, y, False), piece(zz, y, False), late_s.at[t], late_r.at[t], pair_dev)

    def last_late():
        return remote(piece(z_at(7), yh, False), piece(z_at(7), yh, False), late_s.at[15], late_r.at[15], under_dev)

    def products(zs, which):
        n = len(zs)
        for a in which:
            total = None
            for b in range(6):
                rows = [pbuf[zz, :, b].reshape(96, 256) for zz in zs]
                lhs = rows[0] if n == 1 else jnp.concatenate(rows, axis=0)
                term = lax.dot_general(lhs, abuf[a, b], (((1,), (1,)), ((), ())), preferred_element_type=jnp.float32)
                total = term if total is None else total + term
            for i, zz in enumerate(zs):
                got = total[96 * i:96 * i + 96].reshape(4, 24, 256)
                if a == 0:
                    part[zz, 0, :, :, 0:256] = got
                elif a == 1:
                    part[zz, 0, :, :, 256:384] = got[:, :, 0:128]
                    part[zz, 1, :, :, 0:128] = got[:, :, 128:256]
                else:
                    part[zz, 1, :, :, 128:384] = got

    def core(t, zz):
        return remote(part.at[zz, 1 - k], crecv.at[zz], core_s.at[t], core_r.at[t], core_dev)

    def quarter(x):
        return x % 2 * 2 + x // 2

    mine = quarter(x)

    def xcopy(t, zz, d):
        to = lax.rem(x + d, NX)
        return remote(part.at[zz, k, quarter(to)], xrecv.at[zz, d - 1], x_s.at[t, d - 1], x_r.at[t, d - 1], dev(x=to))

    def owned_here(zz):
        return (zz // 4 == x) & (x % 2 == yl) & ((zz // 2) % 2 == k)

    def fcopy(t, zz):
        h, rh = zz % 2, x // 2
        return remote(part.at[zz, k, mine], frecv.at[h, rh, yl, k], f_s.at[t], f_r.at[h, rh, yl, k],
                      dev(x=zz // 4, yl=x % 2, k=(zz // 2) % 2))

    def stage_c(t, zz):
        core(t, zz).wait_recv()
        part[zz, k] = part[zz, k] + crecv[zz]
        for d in (2, 1, 3):
            xcopy(t, zz, d).start()

    def stage_s(t, zz):
        for d in (2, 1, 3):
            xcopy(t, zz, d).wait_recv()
        part[zz, k, mine] = part[zz, k, mine] + xrecv[zz, 0] + xrecv[zz, 1] + xrecv[zz, 2]

        @pl.when(owned_here(zz))
        def _():
            frecv[zz % 2, x // 2, yl, k] = part[zz, k, mine]

        @pl.when(jnp.logical_not(owned_here(zz)))
        def _():
            fcopy(t, zz).start()

    def z_of(t):
        s = (t + 1) // 2
        return lax.rem(z + jnp.where(t % 2 == 1, -s, s) + NZ, NZ)

    def items(s):
        if isinstance(s, int):
            if s == 0:
                return [(0, z)]
            if s == 8:
                return [(15, z_at(8))]
        return [(2 * s - 1, z_at(-s)), (2 * s, z_at(s))]

    def run(stage, s):
        if isinstance(s, int):
            for t, zz in items(s) if s >= 0 else []:
                stage(t, zz)
            return
        for t, zz in items(s):
            @pl.when(t >= 0)
            def _(t=t, zz=zz):
                stage(t, lax.rem(zz + NZ, NZ))

    def when(s, do):
        if isinstance(s, int):
            if s < 7:
                do()
        else:
            pl.when(s < 7)(do)

    def pass_both(s, h, up_on, dn_on):
        below, above = z_at(-s), z_at(s)
        up(s, h, below).wait_recv()
        if up_on:
            up(s + 1, h, below).start()
        else:
            when(s, up(s + 1, h, below).start)
        dn(s, h, above).wait_recv()
        if dn_on:
            dn(s + 1, h, above).start()
        else:
            when(s, dn(s + 1, h, above).start)

    def multiply(*steps):
        pairs = [item for s in steps for item in items(s)]
        for t, zz in pairs:
            late(t, zz, 1 - yh).wait_recv()
        products([zz for _, zz in pairs], range(3))
        for t, zz in pairs:
            core(t, zz).start()

    def step(s):
        pass_both(s, 0, True, False)
        if not isinstance(s, int):
            pl.when(s == 7)(last_late().start)
        for t, zz in items(s):
            late(t, zz, yh).start()
        run(stage_c, s - 2)
        pass_both(s, 1, False, True)
        pass_both(s, 2, True, False)
        multiply(s - 1)
        run(stage_s, s - 3)

    for h in range(2):
        up(1, h, z).start()
        dn(1, h, z).start()
        if h == 0:
            pair(yh).start()
    late(0, z, yh).start()
    tell(0)
    pair(1 - yh).wait_recv()
    up(1, 2, z).start()
    dn(1, 2, z).start()
    loads[3].wait()
    learn(0)
    tell(1)
    learn(1)
    tell(2)
    step(1)
    learn(2)

    @pl.loop(2, 8)
    def _(s):
        step(s)

    up(8, 0, z_at(8)).wait_recv()
    run(stage_c, 6)
    dn(8, 1, z_at(8)).wait_recv()
    up(8, 2, z_at(8)).wait_recv()
    run(stage_s, 5)
    multiply(7, 8)
    run(stage_c, 7)
    run(stage_c, 8)
    run(stage_s, 6)
    pair(yh).wait_send()

    @pl.loop(1, 8)
    def _(s):
        for h in range(3):
            up(s, h, z).wait_send()
            dn(s, h, z).wait_send()

    @pl.loop(0, 15)
    def _(t):
        late(t, z, yh).wait_send()

    last_late().wait_send()
    up(8, 0, z).wait_send()
    up(8, 2, z).wait_send()
    dn(8, 1, z).wait_send()

    @pl.loop(0, 16)
    def _(t):
        core(t, z_of(t)).wait_send()

    run(stage_s, 7)
    run(stage_s, 8)

    @pl.loop(0, 16)
    def _(t):
        for d in (1, 2, 3):
            xcopy(t, z_of(t), d).wait_send()

    masks = supernode_masks(widths_ref, col * 96, (96, 256))
    keeps = [keep_of(masks, struct_ref, a * nprow + row) for a in range(3)]
    for h in range(2):
        zz = 4 * x + 2 * k + h
        halves = []
        for rh in range(2):
            for ys in range(2):
                for ks in range(2):
                    here = (x == 2 * rh + yl) & (ys == yl) & (ks == k)

                    @pl.when(jnp.logical_not(here))
                    def _(rh=rh, ys=ys, ks=ks):
                        remote(frecv.at[h, rh, ys, ks], frecv.at[h, rh, ys, ks], f_s.at[0], f_r.at[h, rh, ys, ks],
                               core_dev).wait_recv()
        halves = [jnp.concatenate([frecv[h, rh, 0, ks] + frecv[h, rh, 1, ks] for rh in range(2)], axis=0) for ks in range(2)]
        lanes = [halves[0][:, 0:256], jnp.concatenate([halves[0][:, 256:384], halves[1][:, 0:128]], axis=1),
                 halves[1][:, 128:384]]
        for a in range(3):
            o_ref[a, 48 * h:48 * h + 48, :] = (-(lanes[a] * keeps[a][48 * h:48 * h + 48])).astype(jnp.bfloat16)

    @pl.loop(0, 16)
    def _(t):
        zz = z_of(t)

        @pl.when(jnp.logical_not(owned_here(zz)))
        def _():
            fcopy(t, zz).wait_send()


def body(ainv, panel, structure, widths):
    a = ainv[:, 0, :, :, 0, :].transpose(0, 2, 1, 3)
    p = panel[:, 0].transpose(0, 2, 1)
    dma, vmem = pltpu.SemaphoreType.DMA, pltpu.VMEM
    f32, bf16 = jnp.float32, jnp.bfloat16
    out = pl.pallas_call(
        kernel,
        out_shape=jax.ShapeDtypeStruct((3, 96, 256), bf16),
        in_specs=[pl.BlockSpec(memory_space=pltpu.HBM)] * 4,
        out_specs=pl.BlockSpec(memory_space=vmem),
        scratch_shapes=[
            pltpu.SMEM((4, 96), jnp.int32), pltpu.SMEM((4,), jnp.int32), vmem((6, 48, 256), bf16),
            vmem((3, 6, 256, 256), bf16),
            vmem((NZ, NY, 6, 48, 256), bf16),
            vmem((NZ, 2, 4, 24, 384), f32),
            vmem((NZ, 4, 24, 384), f32),
            vmem((NZ, 3, 24, 384), f32),
            vmem((2, 2, 2, 2, 24, 384), f32),
            dma((4,)), dma, dma, dma((9, 3)), dma((9, 3)), dma((9, 3)), dma((9, 3)),
            dma((16,)), dma((16,)), dma((16,)), dma((16,)), dma((16, 3)), dma((16, 3)),
            dma((16,)), dma((2, 2, 2, 2)), pltpu.SemaphoreType.REGULAR((3,)),
        ],
        compiler_params=pltpu.CompilerParams(
            collective_id=0, has_side_effects=True, vmem_limit_bytes=32 << 20),
        name="gather_multiply_scatter",
    )(*(pltpu.with_memory_space_constraint(v, pltpu.HBM) for v in (structure, widths, p, a)))
    return out.transpose(0, 2, 1)[:, None]


def solution(mesh):
    in_specs = (P(None, "prow", None, None, "pcol", None), P(None, "pcol", None, "prow"), P(), P())
    out_specs = P(None, "prow", None, "pcol")
    return jax.shard_map(body, mesh=mesh, in_specs=in_specs, out_specs=out_specs, check_vma=False)
```
